32 devices in a mesh: gx: 8 (over y, x, core), gy: 4 (over z).
Axes of the slice: x: 2, y: 2, z: 4, core: 2. Of those that a mesh axis runs over, the one named last changes fastest.
Arguments:
- control: float32 [3, 64, 256, 1024], P(None, None, 'gy', 'gx')
- spread: float32 [3, 256, 1024], P(None, 'gy', 'gx'), may hold values from 0.5 to 2
- kernel_east: float32 [3, 9], replicated, may hold values from -1.5 to 1.5
- kernel_north: float32 [3, 9], replicated, may hold values from -1.5 to 1.5
- vertical: float32 [3, 64, 64], replicated, may hold values from -0.75 to 0.75
- tile_owner: int32 [16384], P(('gx', 'gy')), may hold values from 0 to 31, as said below
- gate_level: int32 [16384], P(('gx', 'gy')), may hold values from 0 to 63
- tile_row: int32 [16384], P(('gx', 'gy')), may hold values from 0 to 63
- beam_azimuth: int32 [16384], P(('gx', 'gy')), may hold values from 80 to 280, as said below
- innovation: float32 [16384, 2, 128], P(('gx', 'gy')), may hold values from -6 to 6
- obs_weight: float32 [16384, 2, 128], P(('gx', 'gy')), may hold values from 0.25 to 4
Outputs:
- gradient: float32 [3, 64, 256, 1024], P(None, None, 'gy', 'gx')
- cost: float32 [2], replicated
The draws below stay inside these ranges and needn't reach their ends.
Inputs may be any that keep to these rules, and one draw needn't show every extreme that they name: `tile_owner`: among the gate rows of one device no tile is named more than 32 times; one tile is named exactly 32 times by the rows of every device. `beam_azimuth`: every azimuth lies within 10 degrees of due east (90) or due west (270).
All inputs are finite; a program needn't handle non-finite values.
Results may differ from the reference program's by a relative error of at most 0.00009.
Values sent between devices are 32-bit elements; how exact they have to be, the bound alone decides.
A program may use at most 192 MiB of HBM per device.

```python
import math
import jax
import jax.numpy as jnp
from jax import lax

FIELDS = 3
NZ = 64
GATES = 128
W = 8
CY = 64
GROW_DEV = 512
CX = 128
TILES = 32
MOST = 32
NX = 1024
NY = 256
GROWS = 16384
N_GX = 8
N_GY = 4


def draw_control(key, part):
    shape = (FIELDS, NZ, NY, NX)
    east = jnp.arange(NX, dtype=jnp.float32) / NX
    north = jnp.arange(NY, dtype=jnp.float32) / NY
    ramp = (0.5 + east)[None, None, None, :] * (0.75 + 0.5 * north)[None, None, :, None]
    base = jax.random.normal(jax.random.fold_in(key, 5), shape, jnp.float32)
    return (base * ramp).astype(jnp.float32)


def draw_tile_owner(key, part):
    base = jax.random.fold_in(key, 11)
    favourite = jax.random.randint(jax.random.fold_in(base, 1), (), 0, TILES)
    block_keys = jax.random.split(jax.random.fold_in(base, 2), TILES)

    def one_block(block_key):
        size_key, order_key, mixing_key = jax.random.split(block_key, 3)
        sizes = jax.random.randint(size_key, (TILES,), MOST // 2, MOST + 1)
        sizes = sizes.at[0].set(MOST)
        bounds = jnp.cumsum(sizes)
        positions = jnp.arange(GROW_DEV, dtype=jnp.int32)
        group = jnp.sum((bounds[None, :] <= positions[:, None]).astype(jnp.int32), axis=1)
        others = jax.random.permutation(order_key, TILES - 1).astype(jnp.int32)
        others = others + (others >= favourite).astype(jnp.int32)
        order = jnp.concatenate([favourite[None].astype(jnp.int32), others])
        chosen = order[group]
        mixing = jax.random.permutation(mixing_key, GROW_DEV)
        return chosen[mixing]
    return jax.vmap(one_block)(block_keys).reshape(GROWS).astype(jnp.int32)


def draw_beam_azimuth(key, part):
    base = jax.random.fold_in(key, 23)
    side = jax.random.randint(jax.random.fold_in(base, 1), (GROWS,), 0, 2)
    offset = jax.random.randint(jax.random.fold_in(base, 2), (GROWS,), 0, 21)
    azimuth = 80 + 180 * side + offset
    azimuth = azimuth.at[0].set(80).at[1].set(280)
    return azimuth.astype(jnp.int32)


def plant(result, key, low, top_value):
    longest = result.shape.index(max(result.shape))
    spots = []
    for shift in (0, 1):
        where = [jax.random.randint(jax.random.fold_in(key, axis), (), 0, length) for axis, length in enumerate(result.shape)]
        where[longest] = (where[longest] + shift) % result.shape[longest]
        spots.append(tuple(where))
    return result.at[spots[0]].set(low).at[spots[1]].set(top_value)


def levels(stream_key, dims, shards, low, largest):
    factor_of = 1.0
    for position, blocks in shards:
        draws = jax.random.uniform(jax.random.fold_in(jax.random.fold_in(stream_key, 6), position), (blocks,), jnp.float32, low / len(shards), largest / len(shards))
        factor_of = factor_of * jnp.repeat(jnp.exp(draws), dims[position] // blocks).reshape((-1,) + (1,) * (len(dims) - 1 - position))
    return factor_of


def centred(key, shape, deviation, limit, cuts=(), kind=jnp.bfloat16):
    entries = jax.random.normal(key, shape, jnp.float32) * deviation
    if len(cuts) > 0:
        entries = levels(key, shape, cuts, -0.22, 0.18) * entries
    return jnp.clip(entries, min=-limit, max=limit).astype(kind)


def setup_inputs(seed: int = 0) -> dict:
    streams_of = jax.random.split(jax.random.key(seed), 12)
    return {
        "control": draw_control(jax.random.fold_in(streams_of[11], 71), 0),
        "spread": jnp.clip(jnp.exp(math.log(2.0) - 1.3862944 * jax.random.uniform(streams_of[1], (FIELDS, NY, NX), jnp.float32) ** levels(streams_of[1], (FIELDS, NY, NX), ((1, 4), (2, 8)), -0.2, 0.2)), 0.5, 2.0),
        "kernel_east": centred(streams_of[2], (FIELDS, W + 1), (2 * W + 1) ** -0.5, 1.5, (), jnp.float32),
        "kernel_north": centred(streams_of[3], (FIELDS, W + 1), (2 * W + 1) ** -0.5, 1.5, (), jnp.float32),
        "vertical": centred(streams_of[4], (FIELDS, NZ, NZ), NZ ** -0.5, 0.75, (), jnp.float32),
        "tile_owner": draw_tile_owner(jax.random.fold_in(streams_of[11], 71), 0),
        "gate_level": plant(jax.random.randint(streams_of[6], (GROWS,), 0, NZ), jax.random.fold_in(streams_of[6], 1), 0, NZ - 1).astype(jnp.int32),
        "tile_row": plant(jax.random.randint(streams_of[7], (GROWS,), 0, CY), jax.random.fold_in(streams_of[7], 1), 0, CY - 1).astype(jnp.int32),
        "beam_azimuth": draw_beam_azimuth(jax.random.fold_in(streams_of[11], 71), 0),
        "innovation": centred(streams_of[9], (GROWS, 2, GATES), 1.0, 6.0, ((0, 32),), jnp.float32),
        "obs_weight": jnp.clip(jnp.exp(math.log(4.0) - 2.7725887 * jax.random.uniform(streams_of[10], (GROWS, 2, GATES), jnp.float32) ** levels(streams_of[10], (GROWS, 2, GATES), ((0, 32),), -0.2, 0.2)), 0.25, 4.0),
    }


def full_taps(kernel):
    return jnp.concatenate([kernel[:, ::-1], kernel[:, 1:]], axis=1)


def filter_axis(field, kernel, axis):
    weights = full_taps(kernel)

    def one_field(pair):
        slab, taps = pair
        widths = [(0, 0), (0, 0), (0, 0)]
        widths[axis - 1] = (W, W)
        padded = jnp.pad(slab, widths)
        length = slab.shape[axis - 1]
        total = jnp.zeros_like(slab)
        for shift in range(2 * W + 1):
            total = total + taps[shift] * lax.slice_in_dim(padded, shift, shift + length, axis=axis - 1)
        return total

    return lax.map(one_field, (field, weights))


def reference(control, spread, kernel_east, kernel_north, vertical, tile_owner, gate_level, tile_row, beam_azimuth, innovation, obs_weight):
    smoothed = filter_axis(filter_axis(control, kernel_east, 3), kernel_north, 2)
    state_field = spread[:, None] * jnp.einsum("fkz,fzyx->fkyx", vertical, smoothed, precision=lax.Precision.HIGHEST)
    blocks = state_field.reshape(FIELDS, NZ, N_GY, CY, N_GX, CX)
    north_index = tile_owner % N_GY
    east_index = tile_owner // N_GY
    picked = blocks[:, gate_level, north_index, tile_row, east_index, :]
    angle = beam_azimuth.astype(jnp.float32) * (2.0 * math.pi / 360.0)
    cosine = jnp.cos(angle)[:, None]
    sine = jnp.sin(angle)[:, None]
    radial = picked[0] * cosine + picked[1] * sine
    modelled = jnp.stack([radial, picked[2]], axis=1)
    departure = modelled - innovation
    weighted = obs_weight * departure
    back_cost = 0.5 * jnp.sum(control * control) / (FIELDS * NZ * NY * NX)
    obs_cost = 0.5 * jnp.sum(weighted * departure) / (2 * GROWS * GATES)
    pushed = jnp.stack([weighted[:, 0] * cosine, weighted[:, 0] * sine, weighted[:, 1]], axis=0)
    adjoint = jnp.zeros((FIELDS, NZ, N_GY, CY, N_GX, CX), jnp.float32)
    adjoint = adjoint.at[:, gate_level, north_index, tile_row, east_index, :].add(pushed)
    adjoint = adjoint.reshape(FIELDS, NZ, NY, NX) * spread[:, None]
    lifted = jnp.einsum("fkz,fkyx->fzyx", vertical, adjoint, precision=lax.Precision.HIGHEST)
    gradient = control + filter_axis(filter_axis(lifted, kernel_east, 3), kernel_north, 2)
    return gradient, jnp.stack([back_cost, obs_cost])
```

```python
import functools
import math

import jax
import jax.numpy as jnp
from jax import lax
from jax.experimental import pallas as pl
from jax.experimental.pallas import tpu as pltpu
from jax.sharding import PartitionSpec as P

F32 = jnp.float32
BF16 = jnp.bfloat16
VMEM_BYTES = 56 * 1024 * 1024


def params():
    return pltpu.CompilerParams(vmem_limit_bytes=VMEM_BYTES)


def split(value):
    high = value.astype(BF16)
    low = (value - high.astype(F32)).astype(BF16)
    return high, low


def doubled(weights):
    high, low = split(weights)
    row = jnp.concatenate([high, low], axis=1)
    return jnp.concatenate([row, row], axis=0)


def times(rows, weights):
    high, low = split(rows)
    both = jnp.dot(
        jnp.concatenate([high, low], axis=1), weights, preferred_element_type=F32
    )
    half = both.shape[1] // 2
    return both[:, :half] + both[:, half:]


def taps_at(kernel_ref, f, distance, allowed):
    total = jnp.zeros(distance.shape, F32)
    for d in range(kernel_ref.shape[1]):
        total = jnp.where(distance == d, kernel_ref[f, d], total)
    return jnp.where(allowed, total, 0.0)


def main_band(kernel_ref, f):
    r = lax.broadcasted_iota(jnp.int32, (128, 128), 0)
    c = lax.broadcasted_iota(jnp.int32, (128, 128), 1)
    return doubled(taps_at(kernel_ref, f, jnp.abs(r - c), jnp.abs(r - c) <= 8))


def rim_band(kernel_ref, f, offset):
    r = (lax.broadcasted_iota(jnp.int32, (128, 128), 0) + (128 - offset)) & 127
    c = (lax.broadcasted_iota(jnp.int32, (128, 128), 1) + (128 - offset)) & 127
    distance = jnp.abs(r - c)
    fits = ((r >> 4) == (c >> 4)) & ((r & 8) != (c & 8)) & (distance <= 8)
    return doubled(taps_at(kernel_ref, f, distance, fits))


def pack_rims(get, put_right, put_left, groups, b):
    lane = lax.broadcasted_iota(jnp.int32, (b, 128), 1)
    first = (lane & 8) == 0

    def one(g, carry):
        even = jnp.zeros((b, 128), F32)
        odd = jnp.zeros((b, 128), F32)
        for q in range(8):
            even = jnp.where(
                (lane >> 4) == q, pltpu.roll(get(16 * g + 2 * q), (16 * q + 8) % 128, 1), even
            )
            odd = jnp.where(
                (((lane + 120) & 127) >> 4) == q,
                pltpu.roll(get(16 * g + 2 * q + 1), (16 * q + 16) % 128, 1),
                odd,
            )
        put_right(g, jnp.where(first, even, odd))
        put_left(g, jnp.where(first, odd, even))
        return carry

    lax.fori_loop(0, groups, one, 0)


def east_filter(get, low_ref, high_ref, put, kernel_ref, f, groups, b):
    band = main_band(kernel_ref, f)
    rim_even = rim_band(kernel_ref, f, 0)
    rim_odd = rim_band(kernel_ref, f, 8)
    lane = lax.broadcasted_iota(jnp.int32, (b, 128), 1)
    first = (lane & 8) == 0
    edge = (lane < 8) | (lane >= 120)

    def one(g, carry):
        low = low_ref[0, g]
        high = high_ref[0, g]
        even = times(jnp.where(first, low, high), rim_even)
        odd = times(jnp.where(first, high, low), rim_odd)
        for q in range(8):
            a = 16 * g + 2 * q
            pair = jnp.concatenate([get(a), get(a + 1)], axis=0)
            flat = times(pair, band)
            put(a, flat[:b] + jnp.where(edge, pltpu.roll(even, (248 - 16 * q) % 128, 1), 0.0))
            put(a + 1, flat[b:] + jnp.where(edge, pltpu.roll(odd, (240 - 16 * q) % 128, 1), 0.0))
        return carry

    lax.fori_loop(0, groups, one, 0)


def north_filter(slab_ref, kernel_ref, f, y0, kb):
    u = slab_ref[pl.ds(y0, 24), pl.ds(kb, 8), :]
    total = kernel_ref[f, 0] * u[8:16]
    for d in range(1, 9):
        total = total + kernel_ref[f, d] * (u[8 - d : 16 - d] + u[8 + d : 16 + d])
    return total


def fold_rows(x):
    return jnp.sum(x.reshape(-1, 8, 128), axis=0)


def rows_kernel(most, owner, level, row, azimuth, inn, wt, out, labels, count):
    rows = owner.shape[0]
    tiles = count.shape[0]
    out[...] = jnp.zeros_like(out)

    def clear(t, carry):
        count[t] = 0
        for j in range(3 * most):
            labels[t * 3 * most + j] = 0
        return carry

    lax.fori_loop(0, tiles, clear, 0)

    def one(i, carry):
        for j in range(4):
            r = i * 4 + j
            o = owner[r]
            rank = count[o]
            count[o] = rank + 1
            at = o * (3 * most) + rank
            labels[at] = level[r]
            labels[at + most] = row[r]
            labels[at + 2 * most] = azimuth[r]
            slot = o * most + rank
            out[slot, 0:2] = inn[r]
            out[slot, 2:4] = wt[r]
        return carry

    lax.fori_loop(0, rows // 4, one, 0)


def pack_rows(owner, level, row, azimuth, inn, wt, tiles, most):
    smem = pl.BlockSpec(memory_space=pltpu.SMEM)
    vmem = pl.BlockSpec(memory_space=pltpu.VMEM)
    return pl.pallas_call(
        functools.partial(rows_kernel, most),
        out_shape=(
            jax.ShapeDtypeStruct((tiles * most, 4, 128), F32),
            jax.ShapeDtypeStruct((tiles * 3 * most,), jnp.int32),
        ),
        in_specs=[smem] * 4 + [vmem] * 2,
        out_specs=(vmem, smem),
        scratch_shapes=[pltpu.SMEM((tiles,), jnp.int32)],
        compiler_params=params(),
        name="pack_rows",
    )(owner, level, row, azimuth, inn, wt)


def rims_kernel(c_ref, right, left, square):
    a, b = c_ref.shape[1], c_ref.shape[2]

    def put_right(g, v):
        right[0, g] = v

    def put_left(g, v):
        left[0, g] = v

    pack_rims(lambda s: c_ref[0, s], put_right, put_left, a // 16, b)

    def one(s, total):
        v = c_ref[0, s]
        return total + fold_rows(v * v)

    square[0] = lax.fori_loop(0, a, one, jnp.zeros((8, 128), F32))


def control_rims(control):
    f, a, b, w = control.shape
    rim = pl.BlockSpec((1, a // 16, b, w), lambda i: (i, 0, 0, 0))
    rim_shape = jax.ShapeDtypeStruct((f, a // 16, b, w), F32)
    return pl.pallas_call(
        rims_kernel,
        grid=(f,),
        in_specs=[pl.BlockSpec((1, a, b, w), lambda i: (i, 0, 0, 0))],
        out_specs=(rim, rim, pl.BlockSpec((1, 8, w), lambda i: (i, 0, 0))),
        out_shape=(rim_shape, rim_shape, jax.ShapeDtypeStruct((f, 8, w), F32)),
        compiler_params=params(),
        name="control_rims",
    )(control)


def forward_kernel(c_ref, low, high, vert, kernel_ref, out, top, bottom, flat):
    f = pl.program_id(0)
    a, b = c_ref.shape[1], c_ref.shape[2]

    def put(s, v):
        flat[pl.ds(pl.multiple_of(s * b, b), b), :] = v

    east_filter(lambda s: c_ref[0, s], low, high, put, kernel_ref, f, a // 16, b)
    v = vert[0]

    def one(p, carry):
        for j in range(4):
            y = p * 8 + 2 * j
            x = jnp.concatenate(
                [flat[pl.ds(y, a, stride=b), :], flat[pl.ds(y + 1, a, stride=b), :]], axis=1
            )
            h, l = split(x)
            r = jnp.dot(v, jnp.concatenate([h, l, h, l], axis=0), preferred_element_type=F32)
            out[0, y] = r[:, :128]
            out[0, y + 1] = r[:, 128:]
        return carry

    lax.fori_loop(0, b // 8, one, 0)
    top[0] = out[0, b - 8 :]
    bottom[0] = out[0, :8]


def forward(control, low, high, vert, kernel_east):
    f, a, b, w = control.shape
    rim = pl.BlockSpec((1, a // 16, b, w), lambda i: (i, 0, 0, 0))
    edge = pl.BlockSpec((1, 8, a, w), lambda i: (i, 0, 0, 0))
    edge_shape = jax.ShapeDtypeStruct((f, 8, a, w), F32)
    return pl.pallas_call(
        forward_kernel,
        grid=(f,),
        in_specs=[
            pl.BlockSpec((1, a, b, w), lambda i: (i, 0, 0, 0)),
            rim,
            rim,
            pl.BlockSpec((1, a, 4 * a), lambda i: (i, 0, 0)),
            pl.BlockSpec(memory_space=pltpu.SMEM),
        ],
        out_specs=(pl.BlockSpec((1, b, a, w), lambda i: (i, 0, 0, 0)), edge, edge),
        out_shape=(jax.ShapeDtypeStruct((f, b, a, w), F32), edge_shape, edge_shape),
        scratch_shapes=[pltpu.VMEM((a * b, w), F32)],
        compiler_params=params(),
        name="forward",
    )(control, low, high, vert, kernel_east)


def observe_kernel(
    cell, cosine, sine, kernel_ref, u_ref, low, high, spread, rows_ref,
    adj, right, left, obs,
    slab, s0, s1, s2, a0, a1, a2, m0, m1,
):
    fields, b, a, w = u_ref.shape
    states = (s0, s1, s2)
    adjs = (a0, a1, a2)
    for f in range(fields):
        slab[0:8] = low[f]
        slab[8 : 8 + b] = u_ref[f]
        slab[8 + b :] = high[f]
        state = states[f]
        grown = adjs[f]

        def one(i, carry):
            y0 = (i // (a // 8)) * 8
            kb = pl.multiple_of((i % (a // 8)) * 8, 8)
            total = north_filter(slab, kernel_ref, f, y0, kb)
            for j in range(8):
                scale = spread[f, pl.ds(y0 + j, 1), :]
                at = pl.multiple_of((y0 + j) * a + kb, 8)
                state[pl.ds(at, 8), :] = total[j] * scale
                grown[pl.ds(at, 8), :] = jnp.zeros((8, w), F32)
            return carry

        lax.fori_loop(0, (b // 8) * (a // 8), one, 0)

    count = rows_ref.shape[0]

    def pick(i, carry):
        for j in range(8):
            r = i * 8 + j
            at = cell[r]
            m0[pl.ds(r, 1), :] = cosine[r] * s0[pl.ds(at, 1), :] + sine[r] * s1[pl.ds(at, 1), :]
            m1[pl.ds(r, 1), :] = s2[pl.ds(at, 1), :]
        return carry

    lax.fori_loop(0, count // 8, pick, 0)

    def weigh(i, total):
        at = pl.ds(pl.multiple_of(i * 8, 8), 8)
        d0 = m0[at, :] - rows_ref[at, 0, :]
        d1 = m1[at, :] - rows_ref[at, 1, :]
        w0 = rows_ref[at, 2, :] * d0
        w1 = rows_ref[at, 3, :] * d1
        m0[at, :] = w0
        m1[at, :] = w1
        return total + (w0 * d0 + w1 * d1)

    obs[...] = lax.fori_loop(0, count // 8, weigh, jnp.zeros((8, w), F32))

    def push(i, carry):
        for j in range(8):
            r = i * 8 + j
            at = pl.ds(cell[r], 1)
            w0 = m0[pl.ds(r, 1), :]
            a0[at, :] = a0[at, :] + cosine[r] * w0
            a1[at, :] = a1[at, :] + sine[r] * w0
            a2[at, :] = a2[at, :] + m1[pl.ds(r, 1), :]
        return carry

    lax.fori_loop(0, count // 8, push, 0)
    for f in range(fields):
        grown = adjs[f]

        def scale_rows(y, carry):
            at = pl.ds(pl.multiple_of(y * a, a), a)
            adj[f, y] = grown[at, :] * spread[f, pl.ds(y, 1), :]
            return carry

        lax.fori_loop(0, b, scale_rows, 0)

        def put_right(g, v):
            right[f, g] = v

        def put_left(g, v):
            left[f, g] = v

        pack_rims(lambda s: adj[f, s], put_right, put_left, b // 16, a)


def observe(cell, cosine, sine, kernel_north, u, low, high, spread, rows):
    f, b, a, w = u.shape
    smem = pl.BlockSpec(memory_space=pltpu.SMEM)
    vmem = pl.BlockSpec(memory_space=pltpu.VMEM)
    rim = jax.ShapeDtypeStruct((f, b // 16, a, w), F32)
    return pl.pallas_call(
        observe_kernel,
        in_specs=[smem] * 4 + [vmem] * 5,
        out_specs=(vmem,) * 4,
        out_shape=(
            jax.ShapeDtypeStruct((f, b, a, w), F32),
            rim,
            rim,
            jax.ShapeDtypeStruct((8, w), F32),
        ),
        scratch_shapes=[pltpu.VMEM((b + 16, a, w), F32)]
        + [pltpu.VMEM((a * b, w), F32)] * 6
        + [pltpu.VMEM((rows.shape[0], w), F32)] * 2,
        compiler_params=params(),
        name="observe",
    )(cell, cosine, sine, kernel_north, u, low, high, spread, rows)


def back_east_kernel(x_ref, low, high, kernel_ref, out, top, bottom):
    f = pl.program_id(0)
    b, a = x_ref.shape[1], x_ref.shape[2]

    def put(s, v):
        out[0, s] = v

    east_filter(lambda s: x_ref[0, s], low, high, put, kernel_ref, f, b // 16, a)
    top[0] = out[0, b - 8 :]
    bottom[0] = out[0, :8]


def back_east(x, low, high, kernel_east):
    f, b, a, w = x.shape
    rim = pl.BlockSpec((1, b // 16, a, w), lambda i: (i, 0, 0, 0))
    edge = pl.BlockSpec((1, 8, a, w), lambda i: (i, 0, 0, 0))
    edge_shape = jax.ShapeDtypeStruct((f, 8, a, w), F32)
    full = pl.BlockSpec((1, b, a, w), lambda i: (i, 0, 0, 0))
    return pl.pallas_call(
        back_east_kernel,
        grid=(f,),
        in_specs=[full, rim, rim, pl.BlockSpec(memory_space=pltpu.SMEM)],
        out_specs=(full, edge, edge),
        out_shape=(jax.ShapeDtypeStruct((f, b, a, w), F32), edge_shape, edge_shape),
        compiler_params=params(),
        name="back_east",
    )(x, low, high, kernel_east)


def gradient_kernel(x_ref, low, high, vert, kernel_ref, c_ref, out, slab, flat):
    f = pl.program_id(0)
    b, a, w = x_ref.shape[1:]
    slab[0:8] = low[0]
    slab[8 : 8 + b] = x_ref[0]
    slab[8 + b :] = high[0]

    def one(i, carry):
        y0 = (i // (a // 8)) * 8
        kb = pl.multiple_of((i % (a // 8)) * 8, 8)
        total = north_filter(slab, kernel_ref, f, y0, kb)
        for j in range(8):
            flat[y0 + j, pl.ds(kb, 8), :] = total[j]
        return carry

    lax.fori_loop(0, (b // 8) * (a // 8), one, 0)
    v = vert[0]

    def two(p, carry):
        for j in range(4):
            y = p * 8 + 2 * j
            x = jnp.concatenate([flat[y], flat[y + 1]], axis=1)
            h, l = split(x)
            r = jnp.dot(v, jnp.concatenate([h, l, h, l], axis=0), preferred_element_type=F32)
            s0 = pl.ds(y, a, stride=b)
            s1 = pl.ds(y + 1, a, stride=b)
            out[0, s0, :] = c_ref[0, s0, :] + r[:, :128]
            out[0, s1, :] = c_ref[0, s1, :] + r[:, 128:]
        return carry

    lax.fori_loop(0, b // 8, two, 0)


def gradient_of(x, low, high, vert, kernel_north, control):
    f, b, a, w = x.shape
    edge = pl.BlockSpec((1, 8, a, w), lambda i: (i, 0, 0, 0))
    flat = pl.BlockSpec((1, a * b, w), lambda i: (i, 0, 0))
    return pl.pallas_call(
        gradient_kernel,
        grid=(f,),
        in_specs=[
            pl.BlockSpec((1, b, a, w), lambda i: (i, 0, 0, 0)),
            edge,
            edge,
            pl.BlockSpec((1, a, 4 * a), lambda i: (i, 0, 0)),
            pl.BlockSpec(memory_space=pltpu.SMEM),
            flat,
        ],
        out_specs=flat,
        out_shape=jax.ShapeDtypeStruct((f, a * b, w), F32),
        scratch_shapes=[pltpu.VMEM((b + 16, a, w), F32), pltpu.VMEM((b, a, w), F32)],
        compiler_params=params(),
        name="gradient",
    )(x, low, high, vert, kernel_north, control.reshape(f, a * b, w)).reshape(control.shape)


def exchange(up, down, axis):
    count = lax.axis_size(axis)
    forward_pairs = [(i, i + 1) for i in range(count - 1)]
    backward = [(t, s) for s, t in forward_pairs]
    return lax.ppermute(up, axis, forward_pairs), lax.ppermute(down, axis, backward)


def vertical_parts(v):
    high = lax.reduce_precision(v, 8, 7)
    low = lax.reduce_precision(v - high, 8, 7)
    return jnp.concatenate([high, high, low, low], axis=2).astype(BF16)


def body(
    control, spread, kernel_east, kernel_north, vertical,
    tile_owner, gate_level, tile_row, beam_azimuth, innovation, obs_weight,
):
    tiles = lax.axis_size("gx") * lax.axis_size("gy")
    most = 2 * tile_owner.shape[0] // tiles
    levels = control.shape[1]
    axes = ("gx", "gy")

    right, left, square = control_rims(control)
    low, high = exchange(right, left, "gx")
    rows, labels = pack_rows(
        tile_owner, gate_level, tile_row, beam_azimuth, innovation, obs_weight, tiles, most
    )
    rows = lax.all_to_all(rows, axes, split_axis=0, concat_axis=0, tiled=True)
    labels = lax.all_to_all(
        labels.reshape(tiles, 3, most), axes, split_axis=0, concat_axis=0, tiled=True
    )
    vert = vertical_parts(vertical)
    vert_back = vertical_parts(jnp.swapaxes(vertical, 1, 2))
    u, top, bottom = forward(control, low, high, vert, kernel_east)
    south, north = exchange(top, bottom, "gy")
    cell = (labels[:, 1] * levels + labels[:, 0]).reshape(-1)
    angle = labels[:, 2].reshape(-1).astype(F32) * (2.0 * math.pi / 360.0)
    adj, right, left, obs = observe(
        cell, jnp.cos(angle), jnp.sin(angle), kernel_north, u, south, north, spread, rows
    )
    parts = jnp.stack([jnp.sum(square), jnp.sum(obs)])
    totals = jnp.sum(lax.all_gather(parts, axes), axis=0)
    counts = jnp.array([control.size * tiles, innovation.size * tiles], F32)
    cost = 0.5 * totals / counts
    low, high = exchange(right, left, "gx")
    g, top, bottom = back_east(adj, low, high, kernel_east)
    south, north = exchange(top, bottom, "gy")
    gradient = gradient_of(g, south, north, vert_back, kernel_north, control)
    return gradient, cost


def solution(mesh):
    both = ("gx", "gy")
    placed = (
        P(None, None, "gy", "gx"),
        P(None, "gy", "gx"),
        P(),
        P(),
        P(),
        P(both),
        P(both),
        P(both),
        P(both),
        P(both, None, None),
        P(both, None, None),
    )
    return jax.shard_map(
        body,
        mesh=mesh,
        in_specs=placed,
        out_specs=(P(None, None, "gy", "gx"), P()),
        check_vma=False,
    )
```

```python
import functools
import math

import jax
import jax.numpy as jnp
from jax import lax
from jax.experimental import pallas as pl
from jax.experimental.pallas import tpu as pltpu
from jax.sharding import PartitionSpec as P

F32 = jnp.float32
BF16 = jnp.bfloat16
VMEM_BYTES = 56 * 1024 * 1024


def params():
    return pltpu.CompilerParams(vmem_limit_bytes=VMEM_BYTES)


def split(value):
    high = value.astype(BF16)
    low = (value - high.astype(F32)).astype(BF16)
    return high, low


def doubled(weights):
    high, low = split(weights)
    row = jnp.concatenate([high, low], axis=1)
    return jnp.concatenate([row, row], axis=0)


def times(rows, weights):
    high, low = split(rows)
    both = jnp.dot(
        jnp.concatenate([high, low], axis=1), weights, preferred_element_type=F32
    )
    half = both.shape[1] // 2
    return both[:, :half] + both[:, half:]


def taps_at(kernel_ref, f, distance, allowed):
    total = jnp.zeros(distance.shape, F32)
    for d in range(kernel_ref.shape[1]):
        total = jnp.where(distance == d, kernel_ref[f, d], total)
    return jnp.where(allowed, total, 0.0)


def main_band(kernel_ref, f):
    r = lax.broadcasted_iota(jnp.int32, (128, 128), 0)
    c = lax.broadcasted_iota(jnp.int32, (128, 128), 1)
    return doubled(taps_at(kernel_ref, f, jnp.abs(r - c), jnp.abs(r - c) <= 8))


def rim_band(kernel_ref, f, offset):
    r = (lax.broadcasted_iota(jnp.int32, (128, 128), 0) + (128 - offset)) & 127
    c = (lax.broadcasted_iota(jnp.int32, (128, 128), 1) + (128 - offset)) & 127
    distance = jnp.abs(r - c)
    fits = ((r >> 4) == (c >> 4)) & ((r & 8) != (c & 8)) & (distance <= 8)
    return doubled(taps_at(kernel_ref, f, distance, fits))


def pack_rims(get, put_right, put_left, groups, b):
    lane = lax.broadcasted_iota(jnp.int32, (b, 128), 1)
    first = (lane & 8) == 0

    def one(g, carry):
        even = jnp.zeros((b, 128), F32)
        odd = jnp.zeros((b, 128), F32)
        for q in range(8):
            even = jnp.where(
                (lane >> 4) == q, pltpu.roll(get(16 * g + 2 * q), (16 * q + 8) % 128, 1), even
            )
            odd = jnp.where(
                (((lane + 120) & 127) >> 4) == q,
                pltpu.roll(get(16 * g + 2 * q + 1), (16 * q + 16) % 128, 1),
                odd,
            )
        put_right(g, jnp.where(first, even, odd))
        put_left(g, jnp.where(first, odd, even))
        return carry

    lax.fori_loop(0, groups, one, 0)


def east_filter(get, low_ref, high_ref, put, kernel_ref, f, groups, b):
    band = main_band(kernel_ref, f)
    rim_even = rim_band(kernel_ref, f, 0)
    rim_odd = rim_band(kernel_ref, f, 8)
    lane = lax.broadcasted_iota(jnp.int32, (b, 128), 1)
    first = (lane & 8) == 0
    edge = (lane < 8) | (lane >= 120)

    def one(g, carry):
        low = low_ref[f, g]
        high = high_ref[f, g]
        even = times(jnp.where(first, low, high), rim_even)
        odd = times(jnp.where(first, high, low), rim_odd)
        for part in range(2):
            many = jnp.concatenate([get(16 * g + 8 * part + j) for j in range(8)], axis=0)
            flat = times(many, band)
            for j in range(4):
                q = 4 * part + j
                at = 16 * g + 2 * q
                own = flat[2 * j * b : (2 * j + 1) * b]
                put(at, own + jnp.where(edge, pltpu.roll(even, (248 - 16 * q) % 128, 1), 0.0))
                own = flat[(2 * j + 1) * b : (2 * j + 2) * b]
                put(at + 1, own + jnp.where(edge, pltpu.roll(odd, (240 - 16 * q) % 128, 1), 0.0))
        return carry

    lax.fori_loop(0, groups, one, 0)


def north_filter(slab_ref, kernel_ref, f, y0, kb):
    u = slab_ref[f, pl.ds(y0, 24), pl.ds(kb, 8), :]
    total = kernel_ref[f, 0] * u[8:16]
    for d in range(1, 9):
        total = total + kernel_ref[f, d] * (u[8 - d : 16 - d] + u[8 + d : 16 + d])
    return total


def fold_rows(x):
    return jnp.sum(x.reshape(-1, 8, 128), axis=0)


def rows_kernel(most, owner, level, row, azimuth, inn, wt, out, labels, count):
    rows = owner.shape[0]
    tiles = count.shape[0]
    out[...] = jnp.zeros_like(out)

    def clear(t, carry):
        count[t] = 0
        for j in range(3 * most):
            labels[t * 3 * most + j] = 0
        return carry

    lax.fori_loop(0, tiles, clear, 0)

    def one(i, carry):
        for j in range(4):
            r = i * 4 + j
            o = owner[r]
            rank = count[o]
            count[o] = rank + 1
            slot = o * most + rank
            labels[slot * 3] = level[r]
            labels[slot * 3 + 1] = row[r]
            labels[slot * 3 + 2] = azimuth[r]
            out[slot, 0:2] = inn[r]
            out[slot, 2:4] = wt[r]
        return carry

    lax.fori_loop(0, rows // 4, one, 0)


def pack_rows(owner, level, row, azimuth, inn, wt, tiles, most):
    smem = pl.BlockSpec(memory_space=pltpu.SMEM)
    vmem = pl.BlockSpec(memory_space=pltpu.VMEM)
    return pl.pallas_call(
        functools.partial(rows_kernel, most),
        out_shape=(
            jax.ShapeDtypeStruct((tiles * most, 4, 128), F32),
            jax.ShapeDtypeStruct((tiles * 3 * most,), jnp.int32),
        ),
        in_specs=[smem] * 4 + [vmem] * 2,
        out_specs=(vmem, smem),
        scratch_shapes=[pltpu.SMEM((tiles,), jnp.int32)],
        compiler_params=params(),
        name="pack_rows",
    )(owner, level, row, azimuth, inn, wt)


def send(src, dst, sems, which, f, axis, target):
    return pltpu.make_async_remote_copy(
        src_ref=src.at[f],
        dst_ref=dst.at[f],
        send_sem=sems.at[0, which, f],
        recv_sem=sems.at[1, which, f],
        device_id={axis: target},
        device_id_type=pl.DeviceIdType.MESH,
    )


def sweep_kernel(
    nx, ny, first, x_ref, east, north, extra, extra2, out, total_out,
    xbuf, right, left, low, high, slab, flat, fill_sems, sems, parts, sum_sems,
):
    fields, a, b, w = x_ref.shape
    ys, ks = slab.shape[1] - 16, slab.shape[2]
    ix = lax.axis_index("gx")
    iy = lax.axis_index("gy")
    up_x, down_x = jnp.minimum(ix + 1, nx - 1), jnp.maximum(ix - 1, 0)
    up_y, down_y = jnp.minimum(iy + 1, ny - 1), jnp.maximum(iy - 1, 0)
    has_up_x, has_down_x = ix < nx - 1, ix > 0
    has_up_y, has_down_y = iy < ny - 1, iy > 0

    def fill(f):
        return pltpu.make_async_copy(x_ref.at[f], xbuf.at[f], fill_sems.at[f])

    for f in range(fields):
        fill(f).start()

    barrier = pltpu.get_barrier_semaphore()

    def greet(axis, peer):
        pl.semaphore_signal(
            barrier, inc=1, device_id={axis: peer}, device_id_type=pl.DeviceIdType.MESH
        )

    if first:
        for axis, peer, there in (
            ("gx", up_x, has_up_x),
            ("gx", down_x, has_down_x),
            ("gy", up_y, has_up_y),
            ("gy", down_y, has_down_y),
        ):

            @pl.when(there)
            def _():
                greet(axis, peer)

        beside = jnp.minimum(ix, 1) + jnp.minimum(nx - 1 - ix, 1)
        around = jnp.minimum(iy, 1) + jnp.minimum(ny - 1 - iy, 1)
        pl.semaphore_wait(barrier, beside + around)
    else:
        for j in range(1, nx):
            greet("gx", lax.rem(ix + j, nx))
        for j in range(1, ny):
            greet("gy", lax.rem(iy + j, ny))
        pl.semaphore_wait(barrier, nx + ny - 2)

    @pl.when(jnp.logical_not(has_down_x))
    def _():
        low[...] = jnp.zeros_like(low)

    @pl.when(jnp.logical_not(has_up_x))
    def _():
        high[...] = jnp.zeros_like(high)

    @pl.when(jnp.logical_not(has_down_y))
    def _():
        slab[:, 0:8] = jnp.zeros((fields, 8, ks, w), F32)

    @pl.when(jnp.logical_not(has_up_y))
    def _():
        slab[:, ys + 8 :] = jnp.zeros((fields, 8, ks, w), F32)

    def to_up_x(f):
        return send(right, low, sems, 0, f, "gx", up_x)

    def to_down_x(f):
        return send(left, high, sems, 1, f, "gx", down_x)

    def edge_copy(f, which, src, dst, target):
        return pltpu.make_async_remote_copy(
            src_ref=slab.at[f, pl.ds(src, 8)],
            dst_ref=slab.at[f, pl.ds(dst, 8)],
            send_sem=sems.at[0, which, f],
            recv_sem=sems.at[1, which, f],
            device_id={"gy": target},
            device_id_type=pl.DeviceIdType.MESH,
        )

    def to_up_y(f):
        return edge_copy(f, 2, ys, 0, up_y)

    def to_down_y(f):
        return edge_copy(f, 3, 8, ys + 8, down_y)

    def share(axis, n, slot, peer, row):
        return pltpu.make_async_remote_copy(
            src_ref=parts.at[row, slot],
            dst_ref=parts.at[row, slot],
            send_sem=sum_sems.at[0, row, peer],
            recv_sem=sum_sems.at[1, row, slot],
            device_id={axis: peer},
            device_id_type=pl.DeviceIdType.MESH,
        )

    def arrival(axis, peer, row):
        return pltpu.make_async_remote_copy(
            src_ref=parts.at[row, peer],
            dst_ref=parts.at[row, peer],
            send_sem=sum_sems.at[0, row, peer],
            recv_sem=sum_sems.at[1, row, peer],
            device_id={axis: peer},
            device_id_type=pl.DeviceIdType.MESH,
        )

    if not first:
        parts[0, ix] = extra[...]
        for j in range(1, nx):
            share("gx", nx, ix, lax.rem(ix + j, nx), 0).start()

    def pack(f, carry):
        fill(f).wait()

        def put_right(g, v):
            right[f, g] = v

        def put_left(g, v):
            left[f, g] = v

        pack_rims(lambda s: xbuf[f, s], put_right, put_left, a // 16, b)

        @pl.when(has_up_x)
        def _():
            to_up_x(f).start()

        @pl.when(has_down_x)
        def _():
            to_down_x(f).start()

        return carry

    lax.fori_loop(0, fields, pack, 0)

    if first:

        def square(i, total):
            v = xbuf[i // a, i % a]
            return total + fold_rows(v * v)

        total_out[...] = lax.fori_loop(0, fields * a, square, jnp.zeros((8, w), F32))
    else:
        for j in range(1, nx):
            arrival("gx", lax.rem(ix + j, nx), 0).wait_recv()
        row_sum = parts[0, 0]
        for j in range(1, nx):
            row_sum = row_sum + parts[0, j]
        parts[1, iy] = row_sum
        for j in range(1, ny):
            share("gy", ny, iy, lax.rem(iy + j, ny), 1).start()

    def middle(f, carry):
        @pl.when(has_down_x)
        def _():
            to_up_x(f).wait_recv()

        @pl.when(has_up_x)
        def _():
            to_down_x(f).wait_recv()

        if first:
            pitch = b + 8

            def put(s, v):
                flat[pl.ds(pl.multiple_of(s * pitch, 8), b), :] = v

            east_filter(lambda s: xbuf[f, s], low, high, put, east, f, a // 16, b)
            v = extra[f]

            def one(p, carry):
                for j in range(4):
                    y = p * 8 + 2 * j
                    x = jnp.concatenate(
                        [flat[pl.ds(y, a, stride=pitch), :], flat[pl.ds(y + 1, a, stride=pitch), :]],
                        axis=1,
                    )
                    h, l = split(x)
                    r = jnp.dot(
                        v, jnp.concatenate([h, l, h, l], axis=0), preferred_element_type=F32
                    )
                    slab[f, 8 + y] = r[:, :w]
                    slab[f, 9 + y] = r[:, w:]
                return carry

            lax.fori_loop(0, b // 8, one, 0)
        else:

            def put_slab(s, v):
                slab[f, 8 + s] = v

            east_filter(lambda s: xbuf[f, s], low, high, put_slab, east, f, a // 16, b)

        @pl.when(has_up_y)
        def _():
            to_up_y(f).start()

        @pl.when(has_down_y)
        def _():
            to_down_y(f).start()

        return carry

    lax.fori_loop(0, fields, middle, 0)

    def last(f, carry):
        @pl.when(has_down_y)
        def _():
            to_up_y(f).wait_recv()

        @pl.when(has_up_y)
        def _():
            to_down_y(f).wait_recv()

        def one(i, carry):
            y0 = (i // (ks // 8)) * 8
            kb = pl.multiple_of((i % (ks // 8)) * 8, 8)
            total = north_filter(slab, north, f, y0, kb)
            for j in range(8):
                value = total[j]
                if first:
                    value = value * extra2[f, pl.ds(y0 + j, 1), :]
                out[f, y0 + j, pl.ds(kb, 8), :] = value
            return carry

        lax.fori_loop(0, (ys // 8) * (ks // 8), one, 0)
        return carry

    lax.fori_loop(0, fields, last, 0)

    if not first:
        for j in range(1, ny):
            arrival("gy", lax.rem(iy + j, ny), 1).wait_recv()
        all_sum = parts[1, 0]
        for j in range(1, ny):
            all_sum = all_sum + parts[1, j]
        total_out[...] = all_sum
        for j in range(1, nx):
            share("gx", nx, ix, lax.rem(ix + j, nx), 0).wait_send()
        for j in range(1, ny):
            share("gy", ny, iy, lax.rem(iy + j, ny), 1).wait_send()

    def drain(f, carry):
        @pl.when(has_up_x)
        def _():
            to_up_x(f).wait_send()

        @pl.when(has_down_x)
        def _():
            to_down_x(f).wait_send()

        @pl.when(has_up_y)
        def _():
            to_up_y(f).wait_send()

        @pl.when(has_down_y)
        def _():
            to_down_y(f).wait_send()

        return carry

    lax.fori_loop(0, fields, drain, 0)


def sweep(first, x, east, north, extra, extra2):
    f, a, b, w = x.shape
    nx, ny = lax.axis_size("gx"), lax.axis_size("gy")
    ys, ks = (b, a) if first else (a, b)
    smem = pl.BlockSpec(memory_space=pltpu.SMEM)
    vmem = pl.BlockSpec(memory_space=pltpu.VMEM)
    rim = pltpu.VMEM((f, a // 16, b, w), F32)
    total = (8, w) if first else (2, 8, w)
    return pl.pallas_call(
        functools.partial(sweep_kernel, nx, ny, first),
        in_specs=[pl.BlockSpec(memory_space=pl.ANY), smem, smem, vmem, vmem],
        out_specs=(vmem, vmem),
        out_shape=(
            jax.ShapeDtypeStruct((f, ys, ks, w), F32),
            jax.ShapeDtypeStruct(total, F32),
        ),
        scratch_shapes=[
            pltpu.VMEM((f, a, b, w), F32),
            rim,
            rim,
            rim,
            rim,
            pltpu.VMEM((f, ys + 16, ks, w), F32),
            pltpu.VMEM((a * (b + 8), w), F32),
            pltpu.SemaphoreType.DMA((f,)),
            pltpu.SemaphoreType.DMA((2, 4, f)),
            pltpu.VMEM((2, max(nx, ny), 2, 8, w), F32),
            pltpu.SemaphoreType.DMA((2, 2, max(nx, ny))),
        ],
        compiler_params=pltpu.CompilerParams(
            vmem_limit_bytes=VMEM_BYTES,
            collective_id=0 if first else 1,
            has_side_effects=True,
        ),
        name="sweep_forward" if first else "sweep_back",
    )(x, east, north, extra, extra2)


def observe_kernel(
    cell, cosine, sine, s_ref, spread, rows_ref, adj, obs, a0, a1, a2, m0, m1
):
    fields, b, w = spread.shape
    a = s_ref.shape[1] // b
    s0, s1, s2 = s_ref.at[0], s_ref.at[1], s_ref.at[2]
    adjs = (a0, a1, a2)
    for f in range(fields):
        adjs[f][...] = jnp.zeros_like(a0)

    count = rows_ref.shape[0]

    def pick(i, carry):
        for j in range(8):
            r = i * 8 + j
            at = cell[r]
            m0[pl.ds(r, 1), :] = cosine[r] * s0[pl.ds(at, 1), :] + sine[r] * s1[pl.ds(at, 1), :]
            m1[pl.ds(r, 1), :] = s2[pl.ds(at, 1), :]
        return carry

    lax.fori_loop(0, count // 8, pick, 0)

    def weigh(i, total):
        at = pl.ds(pl.multiple_of(i * 8, 8), 8)
        d0 = m0[at, :] - rows_ref[at, 0, :]
        d1 = m1[at, :] - rows_ref[at, 1, :]
        w0 = rows_ref[at, 2, :] * d0
        w1 = rows_ref[at, 3, :] * d1
        m0[at, :] = w0
        m1[at, :] = w1
        return total + (w0 * d0 + w1 * d1)

    obs[...] = lax.fori_loop(0, count // 8, weigh, jnp.zeros((8, w), F32))

    def push(i, carry):
        for j in range(8):
            r = i * 8 + j
            at = pl.ds(cell[r], 1)
            w0 = m0[pl.ds(r, 1), :]
            a0[at, :] = a0[at, :] + cosine[r] * w0
            a1[at, :] = a1[at, :] + sine[r] * w0
            a2[at, :] = a2[at, :] + m1[pl.ds(r, 1), :]
        return carry

    lax.fori_loop(0, count // 8, push, 0)
    for f in range(fields):
        grown = adjs[f]

        def scale_rows(y, carry):
            at = pl.ds(pl.multiple_of(y * a, a), a)
            adj[f, y] = grown[at, :] * spread[f, pl.ds(y, 1), :]
            return carry

        lax.fori_loop(0, b, scale_rows, 0)


def observe(cell, cosine, sine, state, spread, rows):
    f, b, w = spread.shape
    cells = state.shape[1]
    smem = pl.BlockSpec(memory_space=pltpu.SMEM)
    vmem = pl.BlockSpec(memory_space=pltpu.VMEM)
    return pl.pallas_call(
        observe_kernel,
        in_specs=[smem] * 3 + [vmem] * 3,
        out_specs=(vmem, vmem),
        out_shape=(
            jax.ShapeDtypeStruct((f, b, cells // b, w), F32),
            jax.ShapeDtypeStruct((8, w), F32),
        ),
        scratch_shapes=[pltpu.VMEM((cells, w), F32)] * 3
        + [pltpu.VMEM((rows.shape[0], w), F32)] * 2,
        compiler_params=params(),
        name="observe",
    )(cell, cosine, sine, state, spread, rows)


def gradient_kernel(x_ref, vert, c_ref, out, flat):
    b, a, w = x_ref.shape[1:]
    pitch = b + 8
    v = vert[0]
    for j in range(b // 2):
        x = jnp.concatenate([x_ref[0, 2 * j], x_ref[0, 2 * j + 1]], axis=1)
        h, l = split(x)
        r = jnp.dot(v, jnp.concatenate([h, l, h, l], axis=0), preferred_element_type=F32)
        flat[pl.ds(2 * j, a, stride=pitch), :] = r[:, :w]
        flat[pl.ds(2 * j + 1, a, stride=pitch), :] = r[:, w:]
    for s in range(a):
        out[0, s] = c_ref[0, s] + flat[s * pitch : s * pitch + b, :]


def gradient_of(x, vert, control):
    f, b, a, w = x.shape
    rows = 16
    tall = pl.BlockSpec((1, a, rows, w), lambda i, j: (i, 0, j, 0))
    return pl.pallas_call(
        gradient_kernel,
        grid=(f, b // rows),
        in_specs=[
            pl.BlockSpec((1, rows, a, w), lambda i, j: (i, j, 0, 0)),
            pl.BlockSpec((1, a, 4 * a), lambda i, j: (i, 0, 0)),
            tall,
        ],
        out_specs=tall,
        out_shape=jax.ShapeDtypeStruct(control.shape, F32),
        scratch_shapes=[pltpu.VMEM((a * (rows + 8), w), F32)],
        compiler_params=params(),
        name="gradient",
    )(x, vert, control)


def vertical_parts(v):
    high = lax.reduce_precision(v, 8, 7)
    low = lax.reduce_precision(v - high, 8, 7)
    return jnp.concatenate([high, high, low, low], axis=2).astype(BF16)


def body(
    control, spread, kernel_east, kernel_north, vertical,
    tile_owner, gate_level, tile_row, beam_azimuth, innovation, obs_weight,
):
    tiles = lax.axis_size("gx") * lax.axis_size("gy")
    most = 2 * tile_owner.shape[0] // tiles
    levels = control.shape[1]
    axes = ("gx", "gy")

    rows, labels = pack_rows(
        tile_owner, gate_level, tile_row, beam_azimuth, innovation, obs_weight, tiles, most
    )
    rows = lax.all_to_all(rows, axes, split_axis=0, concat_axis=0, tiled=True)
    labels = lax.all_to_all(
        labels.reshape(tiles * most, 3), axes, split_axis=0, concat_axis=0, tiled=True
    )
    vert = vertical_parts(vertical)
    vert_back = vertical_parts(jnp.swapaxes(vertical, 1, 2))
    state, square = sweep(True, control, kernel_east, kernel_north, vert, spread)
    cell = labels[:, 1] * levels + labels[:, 0]
    angle = labels[:, 2].astype(F32) * (2.0 * math.pi / 360.0)
    adj, obs = observe(
        cell,
        jnp.cos(angle),
        jnp.sin(angle),
        state.reshape(state.shape[0], -1, state.shape[3]),
        spread,
        rows,
    )
    parts = jnp.stack([square, obs])
    smooth, totals = sweep(False, adj, kernel_east, kernel_north, parts, spread)
    counts = jnp.array([control.size * tiles, innovation.size * tiles], F32)
    cost = 0.5 * jnp.sum(totals, axis=(1, 2)) / counts
    return gradient_of(smooth, vert_back, control), cost


def solution(mesh):
    both = ("gx", "gy")
    placed = (
        P(None, None, "gy", "gx"),
        P(None, "gy", "gx"),
        P(),
        P(),
        P(),
        P(both),
        P(both),
        P(both),
        P(both),
        P(both, None, None),
        P(both, None, None),
    )
    return jax.shard_map(
        body,
        mesh=mesh,
        in_specs=placed,
        out_specs=(P(None, None, "gy", "gx"), P()),
        check_vma=False,
    )
```

```python
import functools
import math

import jax
import jax.numpy as jnp
from jax import lax
from jax.experimental import pallas as pl
from jax.experimental.pallas import tpu as pltpu
from jax.sharding import PartitionSpec as P

F32 = jnp.float32
BF16 = jnp.bfloat16
VMEM_BYTES = 56 * 1024 * 1024


def params():
    return pltpu.CompilerParams(vmem_limit_bytes=VMEM_BYTES)


def split(value):
    high = value.astype(BF16)
    low = (value - high.astype(F32)).astype(BF16)
    return high, low


def doubled(weights):
    high, low = split(weights)
    row = jnp.concatenate([high, low], axis=1)
    return jnp.concatenate([row, row], axis=0)


def times(rows, weights):
    high, low = split(rows)
    both = jnp.dot(
        jnp.concatenate([high, low], axis=1), weights, preferred_element_type=F32
    )
    half = both.shape[1] // 2
    return both[:, :half] + both[:, half:]


def taps_at(kernel_ref, f, distance, allowed):
    total = jnp.zeros(distance.shape, F32)
    for d in range(kernel_ref.shape[1]):
        total = jnp.where(distance == d, kernel_ref[f, d], total)
    return jnp.where(allowed, total, 0.0)


def main_band(kernel_ref, f):
    r = lax.broadcasted_iota(jnp.int32, (128, 128), 0)
    c = lax.broadcasted_iota(jnp.int32, (128, 128), 1)
    return doubled(taps_at(kernel_ref, f, jnp.abs(r - c), jnp.abs(r - c) <= 8))


def rim_band(kernel_ref, f, offset):
    r = (lax.broadcasted_iota(jnp.int32, (128, 128), 0) + (128 - offset)) & 127
    c = (lax.broadcasted_iota(jnp.int32, (128, 128), 1) + (128 - offset)) & 127
    distance = jnp.abs(r - c)
    fits = ((r >> 4) == (c >> 4)) & ((r & 8) != (c & 8)) & (distance <= 8)
    return doubled(taps_at(kernel_ref, f, distance, fits))


def pack_rims(get, put_right, put_left, groups, b):
    lane = lax.broadcasted_iota(jnp.int32, (b, 128), 1)
    first = (lane & 8) == 0

    def one(g, carry):
        even = jnp.zeros((b, 128), F32)
        odd = jnp.zeros((b, 128), F32)
        for q in range(8):
            even = jnp.where(
                (lane >> 4) == q, pltpu.roll(get(16 * g + 2 * q), (16 * q + 8) % 128, 1), even
            )
            odd = jnp.where(
                (((lane + 120) & 127) >> 4) == q,
                pltpu.roll(get(16 * g + 2 * q + 1), (16 * q + 16) % 128, 1),
                odd,
            )
        put_right(g, jnp.where(first, even, odd))
        put_left(g, jnp.where(first, odd, even))
        return carry

    lax.fori_loop(0, groups, one, 0)


def east_filter(get, low_ref, high_ref, put, kernel_ref, f, groups, b):
    band = main_band(kernel_ref, f)
    rim_even = rim_band(kernel_ref, f, 0)
    rim_odd = rim_band(kernel_ref, f, 8)
    lane = lax.broadcasted_iota(jnp.int32, (b, 128), 1)
    first = (lane & 8) == 0
    edge = (lane < 8) | (lane >= 120)

    def one(g, carry):
        low = low_ref[f, g]
        high = high_ref[f, g]
        even = times(jnp.where(first, low, high), rim_even)
        odd = times(jnp.where(first, high, low), rim_odd)
        for part in range(2):
            many = jnp.concatenate([get(16 * g + 8 * part + j) for j in range(8)], axis=0)
            flat = times(many, band)
            for j in range(4):
                q = 4 * part + j
                at = 16 * g + 2 * q
                own = flat[2 * j * b : (2 * j + 1) * b]
                put(at, own + jnp.where(edge, pltpu.roll(even, (248 - 16 * q) % 128, 1), 0.0))
                own = flat[(2 * j + 1) * b : (2 * j + 2) * b]
                put(at + 1, own + jnp.where(edge, pltpu.roll(odd, (240 - 16 * q) % 128, 1), 0.0))
        return carry

    lax.fori_loop(0, groups, one, 0)


def north_filter(slab_ref, kernel_ref, f, y0, kb):
    u = slab_ref[pl.ds(y0, 24), pl.ds(kb, 8), :]
    total = kernel_ref[f, 0] * u[8:16]
    for d in range(1, 9):
        total = total + kernel_ref[f, d] * (u[8 - d : 16 - d] + u[8 + d : 16 + d])
    return total


def mix_levels(parts, pair):
    high, low = split(pair)
    both = jnp.dot(parts, jnp.concatenate([high, low], axis=0), preferred_element_type=F32)
    half = both.shape[0] // 2
    return both[:half] + both[half:]


def fold_rows(x):
    return jnp.sum(x.reshape(-1, 8, 128), axis=0)


def rows_kernel(most, owner, level, row, azimuth, inn, wt, out, count):
    rows = owner.shape[0]
    tiles = count.shape[0]
    out[...] = jnp.zeros_like(out)
    lane = lax.broadcasted_iota(jnp.int32, (4, 128), 1)
    part = lax.broadcasted_iota(jnp.int32, (4, 128), 0)

    def clear(t, carry):
        count[t] = 0
        return carry

    lax.fori_loop(0, tiles, clear, 0)

    def one(i, carry):
        for j in range(8):
            r = i * 8 + j
            o = owner[r]
            rank = count[o]
            count[o] = rank + 1
            base = o * (most + 1)
            label = jnp.where(part == 0, level[r], jnp.where(part == 1, row[r], azimuth[r]))
            out[base + most] = jnp.where(lane == rank, label.astype(F32), out[base + most])
            out[base + rank, 0:2] = inn[r]
            out[base + rank, 2:4] = wt[r]
        return carry

    lax.fori_loop(0, rows // 8, one, 0)


def pack_rows(owner, level, row, azimuth, inn, wt, tiles, most):
    smem = pl.BlockSpec(memory_space=pltpu.SMEM)
    vmem = pl.BlockSpec(memory_space=pltpu.VMEM)
    return pl.pallas_call(
        functools.partial(rows_kernel, most),
        out_shape=jax.ShapeDtypeStruct((tiles * (most + 1), 4, 128), F32),
        in_specs=[smem] * 4 + [vmem] * 2,
        out_specs=vmem,
        scratch_shapes=[pltpu.SMEM((tiles,), jnp.int32)],
        compiler_params=params(),
        name="pack_rows",
    )(owner, level, row, azimuth, inn, wt)


def send(src, dst, sems, which, f, axis, target):
    return pltpu.make_async_remote_copy(
        src_ref=src.at[f],
        dst_ref=dst.at[f],
        send_sem=sems.at[0, which, f],
        recv_sem=sems.at[1, which, f],
        device_id={axis: target},
        device_id_type=pl.DeviceIdType.MESH,
    )


def sweep_kernel(
    nx, ny, first, x_ref, east, north, extra, extra2, out, total_out,
    xbuf, mid, fbuf, right, left, low, high, fill_sems, sems, parts, sum_sems,
):
    fields, _, _, w = x_ref.shape
    ys, ks = out.shape[1], out.shape[2]
    ix = lax.axis_index("gx")
    iy = lax.axis_index("gy")
    up_x, down_x = jnp.minimum(ix + 1, nx - 1), jnp.maximum(ix - 1, 0)
    up_y, down_y = jnp.minimum(iy + 1, ny - 1), jnp.maximum(iy - 1, 0)
    has_up_x, has_down_x = ix < nx - 1, ix > 0
    has_up_y, has_down_y = iy < ny - 1, iy > 0

    def north_rows(ref, f, start, size):
        if first:
            return ref.at[f, :, pl.ds(start, size)]
        return ref.at[f, pl.ds(start, size)]

    def fill(f):
        return pltpu.make_async_copy(
            x_ref.at[f], north_rows(xbuf, f, 8, ys), fill_sems.at[f]
        )

    for f in range(fields):
        fill(f).start()

    barrier = pltpu.get_barrier_semaphore()

    def greet(axis, peer):
        pl.semaphore_signal(
            barrier, inc=1, device_id={axis: peer}, device_id_type=pl.DeviceIdType.MESH
        )

    if first:
        for axis, peer, there in (
            ("gx", up_x, has_up_x),
            ("gx", down_x, has_down_x),
            ("gy", up_y, has_up_y),
            ("gy", down_y, has_down_y),
        ):

            @pl.when(there)
            def _():
                greet(axis, peer)

        beside = jnp.minimum(ix, 1) + jnp.minimum(nx - 1 - ix, 1)
        around = jnp.minimum(iy, 1) + jnp.minimum(ny - 1 - iy, 1)
        pl.semaphore_wait(barrier, beside + around)
    else:
        for j in range(1, nx):
            greet("gx", lax.rem(ix + j, nx))
        for j in range(1, ny):
            greet("gy", lax.rem(iy + j, ny))
        pl.semaphore_wait(barrier, nx + ny - 2)

    @pl.when(jnp.logical_not(has_down_x))
    def _():
        low[...] = jnp.zeros_like(low)

    @pl.when(jnp.logical_not(has_up_x))
    def _():
        high[...] = jnp.zeros_like(high)

    @pl.when(jnp.logical_not(has_down_y))
    def _():
        for f in range(fields):
            edge = north_rows(xbuf, f, 0, 8)
            edge[...] = jnp.zeros(edge.shape, F32)

    @pl.when(jnp.logical_not(has_up_y))
    def _():
        for f in range(fields):
            edge = north_rows(xbuf, f, ys + 8, 8)
            edge[...] = jnp.zeros(edge.shape, F32)

    def to_up_x(f):
        return send(right, low, sems, 0, f, "gx", up_x)

    def to_down_x(f):
        return send(left, high, sems, 1, f, "gx", down_x)

    def edge_copy(f, which, src, dst, target):
        return pltpu.make_async_remote_copy(
            src_ref=north_rows(x_ref, f, src, 8),
            dst_ref=north_rows(xbuf, f, dst, 8),
            send_sem=sems.at[0, which, f],
            recv_sem=sems.at[1, which, f],
            device_id={"gy": target},
            device_id_type=pl.DeviceIdType.MESH,
        )

    def to_up_y(f):
        return edge_copy(f, 2, ys - 8, 0, up_y)

    def to_down_y(f):
        return edge_copy(f, 3, 0, ys + 8, down_y)

    def start_north(f, carry):
        @pl.when(has_up_y)
        def _():
            to_up_y(f).start()

        @pl.when(has_down_y)
        def _():
            to_down_y(f).start()

        return carry

    lax.fori_loop(0, fields, start_north, 0)

    def share(axis, n, slot, peer, row):
        return pltpu.make_async_remote_copy(
            src_ref=parts.at[row, slot],
            dst_ref=parts.at[row, slot],
            send_sem=sum_sems.at[0, row, peer],
            recv_sem=sum_sems.at[1, row, slot],
            device_id={axis: peer},
            device_id_type=pl.DeviceIdType.MESH,
        )

    def arrival(axis, peer, row):
        return pltpu.make_async_remote_copy(
            src_ref=parts.at[row, peer],
            dst_ref=parts.at[row, peer],
            send_sem=sum_sems.at[0, row, peer],
            recv_sem=sum_sems.at[1, row, peer],
            device_id={axis: peer},
            device_id_type=pl.DeviceIdType.MESH,
        )

    if not first:
        parts[0, ix] = extra[...]
        for j in range(1, nx):
            share("gx", nx, ix, lax.rem(ix + j, nx), 0).start()

    def fill_wait(f, carry):
        fill(f).wait()
        return carry

    lax.fori_loop(0, fields, fill_wait, 0)

    if first:

        def square(i, total):
            v = xbuf[i // ks, i % ks, pl.ds(8, ys)]
            return total + fold_rows(v * v)

        total_out[...] = lax.fori_loop(0, fields * ks, square, jnp.zeros((8, w), F32))
    else:
        for j in range(1, nx):
            arrival("gx", lax.rem(ix + j, nx), 0).wait_recv()
        row_sum = parts[0, 0]
        for j in range(1, nx):
            row_sum = row_sum + parts[0, j]
        parts[1, iy] = row_sum
        for j in range(1, ny):
            share("gy", ny, iy, lax.rem(iy + j, ny), 1).start()

    def stage_north(f, carry):
        @pl.when(has_down_y)
        def _():
            to_up_y(f).wait_recv()

        @pl.when(has_up_y)
        def _():
            to_down_y(f).wait_recv()

        if first:
            pitch = ys + 16
            rows_of = xbuf.reshape(fields * ks * pitch, w)
            v = extra[f]

            def one(p, carry):
                for j in range(4):
                    y = p * 8 + 2 * j
                    at = f * (ks * pitch) + y
                    x = jnp.concatenate(
                        [
                            rows_of[pl.ds(at, ks, stride=pitch), :],
                            rows_of[pl.ds(at + 1, ks, stride=pitch), :],
                        ],
                        axis=1,
                    )
                    r = mix_levels(v, x)
                    mid[y] = r[:, :w]
                    mid[y + 1] = r[:, w:]
                return carry

            lax.fori_loop(0, pitch // 8, one, 0)
            slab = mid
        else:
            slab = xbuf.at[f]

        def two(i, carry):
            y0 = (i // (ks // 8)) * 8
            kb = pl.multiple_of((i % (ks // 8)) * 8, 8)
            fbuf[f, pl.ds(y0, 8), pl.ds(kb, 8), :] = north_filter(slab, north, f, y0, kb)
            return carry

        lax.fori_loop(0, (ys // 8) * (ks // 8), two, 0)

        def put_right(g, v):
            right[f, g] = v

        def put_left(g, v):
            left[f, g] = v

        pack_rims(lambda s: fbuf[f, s], put_right, put_left, ys // 16, ks)

        @pl.when(has_up_x)
        def _():
            to_up_x(f).start()

        @pl.when(has_down_x)
        def _():
            to_down_x(f).start()

        return carry

    lax.fori_loop(0, fields, stage_north, 0)

    def stage_east(f, carry):
        @pl.when(has_down_x)
        def _():
            to_up_x(f).wait_recv()

        @pl.when(has_up_x)
        def _():
            to_down_x(f).wait_recv()

        def put(s, v):
            if first:
                v = v * extra2[f, pl.ds(s, 1), :]
            out[f, s] = v

        east_filter(lambda s: fbuf[f, s], low, high, put, east, f, ys // 16, ks)
        return carry

    lax.fori_loop(0, fields, stage_east, 0)

    if not first:
        for j in range(1, ny):
            arrival("gy", lax.rem(iy + j, ny), 1).wait_recv()
        all_sum = parts[1, 0]
        for j in range(1, ny):
            all_sum = all_sum + parts[1, j]
        total_out[...] = all_sum
        for j in range(1, nx):
            share("gx", nx, ix, lax.rem(ix + j, nx), 0).wait_send()
        for j in range(1, ny):
            share("gy", ny, iy, lax.rem(iy + j, ny), 1).wait_send()

    def drain(f, carry):
        @pl.when(has_up_x)
        def _():
            to_up_x(f).wait_send()

        @pl.when(has_down_x)
        def _():
            to_down_x(f).wait_send()

        @pl.when(has_up_y)
        def _():
            to_up_y(f).wait_send()

        @pl.when(has_down_y)
        def _():
            to_down_y(f).wait_send()

        return carry

    lax.fori_loop(0, fields, drain, 0)


def sweep(first, x, east, north, extra, extra2):
    f, a, b, w = x.shape
    nx, ny = lax.axis_size("gx"), lax.axis_size("gy")
    ys, ks = (b, a) if first else (a, b)
    smem = pl.BlockSpec(memory_space=pltpu.SMEM)
    vmem = pl.BlockSpec(memory_space=pltpu.VMEM)
    rim = pltpu.VMEM((f, ys // 16, ks, w), F32)
    total = (8, w) if first else (2, 8, w)
    wide = (f, a, b + 16, w) if first else (f, a + 16, b, w)
    return pl.pallas_call(
        functools.partial(sweep_kernel, nx, ny, first),
        in_specs=[pl.BlockSpec(memory_space=pl.ANY), smem, smem, vmem, vmem],
        out_specs=(vmem, vmem),
        out_shape=(
            jax.ShapeDtypeStruct((f, ys, ks, w), F32),
            jax.ShapeDtypeStruct(total, F32),
        ),
        scratch_shapes=[
            pltpu.VMEM(wide, F32),
            pltpu.VMEM((ys + 16, ks, w), F32),
            pltpu.VMEM((f, ys, ks, w), F32),
            rim,
            rim,
            rim,
            rim,
            pltpu.SemaphoreType.DMA((f,)),
            pltpu.SemaphoreType.DMA((2, 4, f)),
            pltpu.VMEM((2, max(nx, ny), 2, 8, w), F32),
            pltpu.SemaphoreType.DMA((2, 2, max(nx, ny))),
        ],
        compiler_params=pltpu.CompilerParams(
            vmem_limit_bytes=VMEM_BYTES,
            collective_id=0 if first else 1,
            has_side_effects=True,
        ),
        name="sweep_forward" if first else "sweep_back",
    )(x, east, north, extra, extra2)


def observe_kernel(
    most, cell, cosine, sine, s_ref, spread, rows_ref, adj, obs, a0, a1, a2, m0, m1
):
    fields, b, w = spread.shape
    a = s_ref.shape[1] // b
    s0, s1, s2 = s_ref.at[0], s_ref.at[1], s_ref.at[2]
    adjs = (a0, a1, a2)
    for f in range(fields):
        adjs[f][...] = jnp.zeros_like(a0)

    count = cell.shape[0]

    def pick(i, carry):
        for j in range(8):
            r = i * 8 + j
            at = cell[r]
            m0[pl.ds(r, 1), :] = cosine[r] * s0[pl.ds(at, 1), :] + sine[r] * s1[pl.ds(at, 1), :]
            m1[pl.ds(r, 1), :] = s2[pl.ds(at, 1), :]
        return carry

    lax.fori_loop(0, count // 8, pick, 0)

    def weigh(i, total):
        at = pl.ds(pl.multiple_of(i * 8, 8), 8)
        first = (i * 8 // most) * (most + 1) + (i * 8) % most
        slot = pl.ds(first, 8)
        d0 = m0[at, :] - rows_ref[slot, 0, :]
        d1 = m1[at, :] - rows_ref[slot, 1, :]
        w0 = rows_ref[slot, 2, :] * d0
        w1 = rows_ref[slot, 3, :] * d1
        m0[at, :] = w0
        m1[at, :] = w1
        return total + (w0 * d0 + w1 * d1)

    obs[...] = lax.fori_loop(0, count // 8, weigh, jnp.zeros((8, w), F32))

    def push(i, carry):
        for j in range(8):
            r = i * 8 + j
            at = pl.ds(cell[r], 1)
            w0 = m0[pl.ds(r, 1), :]
            a0[at, :] = a0[at, :] + cosine[r] * w0
            a1[at, :] = a1[at, :] + sine[r] * w0
            a2[at, :] = a2[at, :] + m1[pl.ds(r, 1), :]
        return carry

    lax.fori_loop(0, count // 8, push, 0)
    for f in range(fields):
        grown = adjs[f]

        def scale_rows(y, carry):
            at = pl.ds(pl.multiple_of(y * a, a), a)
            adj[f, y] = grown[at, :] * spread[f, pl.ds(y, 1), :]
            return carry

        lax.fori_loop(0, b, scale_rows, 0)


def observe(cell, cosine, sine, state, spread, rows, most):
    f, b, w = spread.shape
    cells = state.shape[1]
    smem = pl.BlockSpec(memory_space=pltpu.SMEM)
    vmem = pl.BlockSpec(memory_space=pltpu.VMEM)
    return pl.pallas_call(
        functools.partial(observe_kernel, most),
        in_specs=[smem] * 3 + [vmem] * 3,
        out_specs=(vmem, vmem),
        out_shape=(
            jax.ShapeDtypeStruct((f, b, cells // b, w), F32),
            jax.ShapeDtypeStruct((8, w), F32),
        ),
        scratch_shapes=[pltpu.VMEM((cells, w), F32)] * 3
        + [pltpu.VMEM((cell.shape[0], w), F32)] * 2,
        compiler_params=params(),
        name="observe",
    )(cell, cosine, sine, state, spread, rows)


def gradient_kernel(x_ref, vert, c_ref, out, flat):
    b, a, w = x_ref.shape[1:]
    pitch = b + 8
    v = vert[0]
    for j in range(b // 2):
        x = jnp.concatenate([x_ref[0, 2 * j], x_ref[0, 2 * j + 1]], axis=1)
        r = mix_levels(v, x)
        flat[pl.ds(2 * j, a, stride=pitch), :] = r[:, :w]
        flat[pl.ds(2 * j + 1, a, stride=pitch), :] = r[:, w:]
    for s in range(a):
        out[0, s] = c_ref[0, s] + flat[s * pitch : s * pitch + b, :]


def gradient_of(x, vert, control):
    f, b, a, w = x.shape
    rows = 16
    tall = pl.BlockSpec((1, a, rows, w), lambda i, j: (i, 0, j, 0))
    return pl.pallas_call(
        gradient_kernel,
        grid=(f, b // rows),
        in_specs=[
            pl.BlockSpec((1, rows, a, w), lambda i, j: (i, j, 0, 0)),
            pl.BlockSpec((1, 2 * a, 2 * a), lambda i, j: (i, 0, 0)),
            tall,
        ],
        out_specs=tall,
        out_shape=jax.ShapeDtypeStruct(control.shape, F32),
        scratch_shapes=[pltpu.VMEM((a * (rows + 8), w), F32)],
        compiler_params=params(),
        name="gradient",
    )(x, vert, control)


def vertical_parts(v):
    high = lax.reduce_precision(v, 8, 7)
    low = lax.reduce_precision(v - high, 8, 7)
    both = jnp.concatenate([high, low], axis=1)
    return jnp.concatenate([both, both], axis=2).astype(BF16)


def body(
    control, spread, kernel_east, kernel_north, vertical,
    tile_owner, gate_level, tile_row, beam_azimuth, innovation, obs_weight,
):
    tiles = lax.axis_size("gx") * lax.axis_size("gy")
    most = 2 * tile_owner.shape[0] // tiles
    levels = control.shape[1]
    axes = ("gx", "gy")

    rows = pack_rows(
        tile_owner, gate_level, tile_row, beam_azimuth, innovation, obs_weight, tiles, most
    )
    rows = lax.all_to_all(rows, axes, split_axis=0, concat_axis=0, tiled=True)
    labels = rows.reshape(tiles, most + 1, 4, -1)[:, most, :3, :most]
    vert = vertical_parts(vertical)
    vert_back = vertical_parts(jnp.swapaxes(vertical, 1, 2))
    state, square = sweep(True, control, kernel_east, kernel_north, vert, spread)
    cell = (labels[:, 1] * levels + labels[:, 0]).astype(jnp.int32).reshape(-1)
    angle = labels[:, 2].reshape(-1) * (2.0 * math.pi / 360.0)
    adj, obs = observe(
        cell,
        jnp.cos(angle),
        jnp.sin(angle),
        state.reshape(state.shape[0], -1, state.shape[3]),
        spread,
        rows,
        most,
    )
    parts = jnp.stack([square, obs])
    smooth, totals = sweep(False, adj, kernel_east, kernel_north, parts, spread)
    counts = jnp.array([control.size * tiles, innovation.size * tiles], F32)
    cost = 0.5 * jnp.sum(totals, axis=(1, 2)) / counts
    return gradient_of(smooth, vert_back, control), cost


def solution(mesh):
    both = ("gx", "gy")
    placed = (
        P(None, None, "gy", "gx"),
        P(None, "gy", "gx"),
        P(),
        P(),
        P(),
        P(both),
        P(both),
        P(both),
        P(both),
        P(both, None, None),
        P(both, None, None),
    )
    return jax.shard_map(
        body,
        mesh=mesh,
        in_specs=placed,
        out_specs=(P(None, None, "gy", "gx"), P()),
        check_vma=False,
    )
```

```python
import functools
import math

import jax
import jax.numpy as jnp
from jax import lax
from jax.experimental import pallas as pl
from jax.experimental.pallas import tpu as pltpu
from jax.sharding import PartitionSpec as P

F32 = jnp.float32
BF16 = jnp.bfloat16
VMEM_BYTES = 56 * 1024 * 1024


def params():
    return pltpu.CompilerParams(vmem_limit_bytes=VMEM_BYTES)


def split(value):
    high = value.astype(BF16)
    low = (value - high.astype(F32)).astype(BF16)
    return high, low


def doubled(weights):
    high, low = split(weights)
    row = jnp.concatenate([high, low], axis=1)
    return jnp.concatenate([row, row], axis=0)


def times(rows, weights):
    high, low = split(rows)
    both = jnp.dot(
        jnp.concatenate([high, low], axis=1), weights, preferred_element_type=F32
    )
    half = both.shape[1] // 2
    return both[:, :half] + both[:, half:]


def taps_at(kernel_ref, f, distance, allowed):
    total = jnp.zeros(distance.shape, F32)
    for d in range(kernel_ref.shape[1]):
        total = jnp.where(distance == d, kernel_ref[f, d], total)
    return jnp.where(allowed, total, 0.0)


def main_band(kernel_ref, f):
    r = lax.broadcasted_iota(jnp.int32, (128, 128), 0)
    c = lax.broadcasted_iota(jnp.int32, (128, 128), 1)
    return doubled(taps_at(kernel_ref, f, jnp.abs(r - c), jnp.abs(r - c) <= 8))


def rim_band(kernel_ref, f, offset):
    r = (lax.broadcasted_iota(jnp.int32, (128, 128), 0) + (128 - offset)) & 127
    c = (lax.broadcasted_iota(jnp.int32, (128, 128), 1) + (128 - offset)) & 127
    distance = jnp.abs(r - c)
    fits = ((r >> 4) == (c >> 4)) & ((r & 8) != (c & 8)) & (distance <= 8)
    return doubled(taps_at(kernel_ref, f, distance, fits))


def pack_rims(get, put_right, put_left, groups, b):
    lane = lax.broadcasted_iota(jnp.int32, (b, 128), 1)
    first = (lane & 8) == 0

    def one(g, carry):
        even = jnp.zeros((b, 128), F32)
        odd = jnp.zeros((b, 128), F32)
        for q in range(8):
            even = jnp.where(
                (lane >> 4) == q, pltpu.roll(get(16 * g + 2 * q), (16 * q + 8) % 128, 1), even
            )
            odd = jnp.where(
                (((lane + 120) & 127) >> 4) == q,
                pltpu.roll(get(16 * g + 2 * q + 1), (16 * q + 16) % 128, 1),
                odd,
            )
        put_right(g, jnp.where(first, even, odd))
        put_left(g, jnp.where(first, odd, even))
        return carry

    lax.fori_loop(0, groups, one, 0)


def east_filter(get, low_ref, high_ref, put, kernel_ref, f, groups, b):
    band = main_band(kernel_ref, f)
    rim_even = rim_band(kernel_ref, f, 0)
    rim_odd = rim_band(kernel_ref, f, 8)
    lane = lax.broadcasted_iota(jnp.int32, (b, 128), 1)
    first = (lane & 8) == 0
    edge = (lane < 8) | (lane >= 120)

    def one(g, carry):
        low = low_ref[f, g]
        high = high_ref[f, g]
        even = times(jnp.where(first, low, high), rim_even)
        odd = times(jnp.where(first, high, low), rim_odd)
        for part in range(2):
            many = jnp.concatenate([get(16 * g + 8 * part + j) for j in range(8)], axis=0)
            flat = times(many, band)
            for j in range(4):
                q = 4 * part + j
                at = 16 * g + 2 * q
                own = flat[2 * j * b : (2 * j + 1) * b]
                put(at, own + jnp.where(edge, pltpu.roll(even, (248 - 16 * q) % 128, 1), 0.0))
                own = flat[(2 * j + 1) * b : (2 * j + 2) * b]
                put(at + 1, own + jnp.where(edge, pltpu.roll(odd, (240 - 16 * q) % 128, 1), 0.0))
        return carry

    lax.fori_loop(0, groups, one, 0)


def north_filter(slab_ref, kernel_ref, f, y0, kb):
    u = slab_ref[f, pl.ds(y0, 24), pl.ds(kb, 8), :]
    total = kernel_ref[f, 0] * u[8:16]
    for d in range(1, 9):
        total = total + kernel_ref[f, d] * (u[8 - d : 16 - d] + u[8 + d : 16 + d])
    return total


def mix_levels(parts, pair):
    high, low = split(pair)
    both = jnp.dot(parts, jnp.concatenate([high, low], axis=0), preferred_element_type=F32)
    half = both.shape[0] // 2
    return both[:half] + both[half:]


def fold_rows(x):
    return jnp.sum(x.reshape(-1, 8, 128), axis=0)


def rows_kernel(most, owner, level, row, azimuth, inn, wt, out, count):
    rows = owner.shape[0]
    tiles = count.shape[0]
    out[...] = jnp.zeros_like(out)
    lane = lax.broadcasted_iota(jnp.int32, (4, 128), 1)
    part = lax.broadcasted_iota(jnp.int32, (4, 128), 0)

    def clear(t, carry):
        count[t] = 0
        return carry

    lax.fori_loop(0, tiles, clear, 0)

    def one(i, carry):
        for j in range(8):
            r = i * 8 + j
            o = owner[r]
            rank = count[o]
            count[o] = rank + 1
            base = o * (most + 1)
            label = jnp.where(part == 0, level[r], jnp.where(part == 1, row[r], azimuth[r]))
            out[base + most] = jnp.where(lane == rank, label.astype(F32), out[base + most])
            out[base + rank, 0:2] = inn[r]
            out[base + rank, 2:4] = wt[r]
        return carry

    lax.fori_loop(0, rows // 8, one, 0)


def pack_rows(owner, level, row, azimuth, inn, wt, tiles, most):
    smem = pl.BlockSpec(memory_space=pltpu.SMEM)
    vmem = pl.BlockSpec(memory_space=pltpu.VMEM)
    return pl.pallas_call(
        functools.partial(rows_kernel, most),
        out_shape=jax.ShapeDtypeStruct((tiles * (most + 1), 4, 128), F32),
        in_specs=[smem] * 4 + [vmem] * 2,
        out_specs=vmem,
        scratch_shapes=[pltpu.SMEM((tiles,), jnp.int32)],
        compiler_params=params(),
        name="pack_rows",
    )(owner, level, row, azimuth, inn, wt)


def send(src, dst, sems, which, f, axis, target):
    return pltpu.make_async_remote_copy(
        src_ref=src.at[f],
        dst_ref=dst.at[f],
        send_sem=sems.at[0, which, f],
        recv_sem=sems.at[1, which, f],
        device_id={axis: target},
        device_id_type=pl.DeviceIdType.MESH,
    )


def sweep_kernel(
    nx, ny, first, x_ref, east, north, extra, extra2, out, total_out,
    xbuf, right, left, low, high, slab, flat, fill_sems, sems, parts, sum_sems,
):
    fields, a, b, w = x_ref.shape
    ys, ks = slab.shape[1] - 16, slab.shape[2]
    ix = lax.axis_index("gx")
    iy = lax.axis_index("gy")
    up_x, down_x = jnp.minimum(ix + 1, nx - 1), jnp.maximum(ix - 1, 0)
    up_y, down_y = jnp.minimum(iy + 1, ny - 1), jnp.maximum(iy - 1, 0)
    has_up_x, has_down_x = ix < nx - 1, ix > 0
    has_up_y, has_down_y = iy < ny - 1, iy > 0

    def fill(f):
        return pltpu.make_async_copy(x_ref.at[f], xbuf.at[f], fill_sems.at[f])

    for f in range(fields):
        fill(f).start()

    barrier = pltpu.get_barrier_semaphore()

    def greet(axis, peer):
        pl.semaphore_signal(
            barrier, inc=1, device_id={axis: peer}, device_id_type=pl.DeviceIdType.MESH
        )

    if first:
        for axis, peer, there in (
            ("gx", up_x, has_up_x),
            ("gx", down_x, has_down_x),
            ("gy", up_y, has_up_y),
            ("gy", down_y, has_down_y),
        ):

            @pl.when(there)
            def _():
                greet(axis, peer)

        beside = jnp.minimum(ix, 1) + jnp.minimum(nx - 1 - ix, 1)
        around = jnp.minimum(iy, 1) + jnp.minimum(ny - 1 - iy, 1)
        pl.semaphore_wait(barrier, beside + around)
    else:
        for j in range(1, nx):
            greet("gx", lax.rem(ix + j, nx))
        for j in range(1, ny):
            greet("gy", lax.rem(iy + j, ny))
        pl.semaphore_wait(barrier, nx + ny - 2)

    @pl.when(jnp.logical_not(has_down_x))
    def _():
        low[...] = jnp.zeros_like(low)

    @pl.when(jnp.logical_not(has_up_x))
    def _():
        high[...] = jnp.zeros_like(high)

    @pl.when(jnp.logical_not(has_down_y))
    def _():
        slab[:, 0:8] = jnp.zeros((fields, 8, ks, w), F32)

    @pl.when(jnp.logical_not(has_up_y))
    def _():
        slab[:, ys + 8 :] = jnp.zeros((fields, 8, ks, w), F32)

    def to_up_x(f):
        return send(right, low, sems, 0, f, "gx", up_x)

    def to_down_x(f):
        return send(left, high, sems, 1, f, "gx", down_x)

    def edge_copy(f, which, src, dst, target):
        return pltpu.make_async_remote_copy(
            src_ref=slab.at[f, pl.ds(src, 8)],
            dst_ref=slab.at[f, pl.ds(dst, 8)],
            send_sem=sems.at[0, which, f],
            recv_sem=sems.at[1, which, f],
            device_id={"gy": target},
            device_id_type=pl.DeviceIdType.MESH,
        )

    def to_up_y(f):
        return edge_copy(f, 2, ys, 0, up_y)

    def to_down_y(f):
        return edge_copy(f, 3, 8, ys + 8, down_y)

    def share(axis, n, slot, peer, row):
        return pltpu.make_async_remote_copy(
            src_ref=parts.at[row, slot],
            dst_ref=parts.at[row, slot],
            send_sem=sum_sems.at[0, row, peer],
            recv_sem=sum_sems.at[1, row, slot],
            device_id={axis: peer},
            device_id_type=pl.DeviceIdType.MESH,
        )

    def arrival(axis, peer, row):
        return pltpu.make_async_remote_copy(
            src_ref=parts.at[row, peer],
            dst_ref=parts.at[row, peer],
            send_sem=sum_sems.at[0, row, peer],
            recv_sem=sum_sems.at[1, row, peer],
            device_id={axis: peer},
            device_id_type=pl.DeviceIdType.MESH,
        )

    if not first:
        parts[0, ix] = extra[...]
        for j in range(1, nx):
            share("gx", nx, ix, lax.rem(ix + j, nx), 0).start()

    def pack(f, carry):
        fill(f).wait()

        def put_right(g, v):
            right[f, g] = v

        def put_left(g, v):
            left[f, g] = v

        pack_rims(lambda s: xbuf[f, s], put_right, put_left, a // 16, b)

        @pl.when(has_up_x)
        def _():
            to_up_x(f).start()

        @pl.when(has_down_x)
        def _():
            to_down_x(f).start()

        return carry

    lax.fori_loop(0, fields, pack, 0)

    if first:

        def square(i, total):
            v = xbuf[i // a, i % a]
            return total + fold_rows(v * v)

        total_out[...] = lax.fori_loop(0, fields * a, square, jnp.zeros((8, w), F32))
    else:
        for j in range(1, nx):
            arrival("gx", lax.rem(ix + j, nx), 0).wait_recv()
        row_sum = parts[0, 0]
        for j in range(1, nx):
            row_sum = row_sum + parts[0, j]
        parts[1, iy] = row_sum
        for j in range(1, ny):
            share("gy", ny, iy, lax.rem(iy + j, ny), 1).start()

    def middle(f, carry):
        @pl.when(has_down_x)
        def _():
            to_up_x(f).wait_recv()

        @pl.when(has_up_x)
        def _():
            to_down_x(f).wait_recv()

        if first:
            pitch = b + 8

            def put(s, v):
                flat[pl.ds(pl.multiple_of(s * pitch, 8), b), :] = v

            east_filter(lambda s: xbuf[f, s], low, high, put, east, f, a // 16, b)
            v = extra[f]

            def one(p, carry):
                for j in range(4):
                    y = p * 8 + 2 * j
                    x = jnp.concatenate(
                        [flat[pl.ds(y, a, stride=pitch), :], flat[pl.ds(y + 1, a, stride=pitch), :]],
                        axis=1,
                    )
                    r = mix_levels(v, x)
                    slab[f, 8 + y] = r[:, :w]
                    slab[f, 9 + y] = r[:, w:]
                return carry

            lax.fori_loop(0, b // 8, one, 0)
        else:

            def put_slab(s, v):
                slab[f, 8 + s] = v

            east_filter(lambda s: xbuf[f, s], low, high, put_slab, east, f, a // 16, b)

        @pl.when(has_up_y)
        def _():
            to_up_y(f).start()

        @pl.when(has_down_y)
        def _():
            to_down_y(f).start()

        return carry

    lax.fori_loop(0, fields, middle, 0)

    def last(f, carry):
        @pl.when(has_down_y)
        def _():
            to_up_y(f).wait_recv()

        @pl.when(has_up_y)
        def _():
            to_down_y(f).wait_recv()

        def one(i, carry):
            y0 = (i // (ks // 8)) * 8
            kb = pl.multiple_of((i % (ks // 8)) * 8, 8)
            total = north_filter(slab, north, f, y0, kb)
            for j in range(8):
                value = total[j]
                if first:
                    value = value * extra2[f, pl.ds(y0 + j, 1), :]
                out[f, y0 + j, pl.ds(kb, 8), :] = value
            return carry

        lax.fori_loop(0, (ys // 8) * (ks // 8), one, 0)
        return carry

    lax.fori_loop(0, fields, last, 0)

    if not first:
        for j in range(1, ny):
            arrival("gy", lax.rem(iy + j, ny), 1).wait_recv()
        all_sum = parts[1, 0]
        for j in range(1, ny):
            all_sum = all_sum + parts[1, j]
        total_out[...] = all_sum
        for j in range(1, nx):
            share("gx", nx, ix, lax.rem(ix + j, nx), 0).wait_send()
        for j in range(1, ny):
            share("gy", ny, iy, lax.rem(iy + j, ny), 1).wait_send()

    def drain(f, carry):
        @pl.when(has_up_x)
        def _():
            to_up_x(f).wait_send()

        @pl.when(has_down_x)
        def _():
            to_down_x(f).wait_send()

        @pl.when(has_up_y)
        def _():
            to_up_y(f).wait_send()

        @pl.when(has_down_y)
        def _():
            to_down_y(f).wait_send()

        return carry

    lax.fori_loop(0, fields, drain, 0)


def sweep(first, x, east, north, extra, extra2):
    f, a, b, w = x.shape
    nx, ny = lax.axis_size("gx"), lax.axis_size("gy")
    ys, ks = (b, a) if first else (a, b)
    smem = pl.BlockSpec(memory_space=pltpu.SMEM)
    vmem = pl.BlockSpec(memory_space=pltpu.VMEM)
    rim = pltpu.VMEM((f, a // 16, b, w), F32)
    total = (8, w) if first else (2, 8, w)
    return pl.pallas_call(
        functools.partial(sweep_kernel, nx, ny, first),
        in_specs=[pl.BlockSpec(memory_space=pl.ANY), smem, smem, vmem, vmem],
        out_specs=(vmem, vmem),
        out_shape=(
            jax.ShapeDtypeStruct((f, ys, ks, w), F32),
            jax.ShapeDtypeStruct(total, F32),
        ),
        scratch_shapes=[
            pltpu.VMEM((f, a, b, w), F32),
            rim,
            rim,
            rim,
            rim,
            pltpu.VMEM((f, ys + 16, ks, w), F32),
            pltpu.VMEM((a * (b + 8), w), F32),
            pltpu.SemaphoreType.DMA((f,)),
            pltpu.SemaphoreType.DMA((2, 4, f)),
            pltpu.VMEM((2, max(nx, ny), 2, 8, w), F32),
            pltpu.SemaphoreType.DMA((2, 2, max(nx, ny))),
        ],
        compiler_params=pltpu.CompilerParams(
            vmem_limit_bytes=VMEM_BYTES,
            collective_id=0 if first else 1,
            has_side_effects=True,
        ),
        name="sweep_forward" if first else "sweep_back",
    )(x, east, north, extra, extra2)


def observe_kernel(
    most, cell, cosine, sine, s_ref, spread, rows_ref, adj, obs, a0, a1, a2, m0, m1
):
    fields, b, w = spread.shape
    a = s_ref.shape[1] // b
    s0, s1, s2 = s_ref.at[0], s_ref.at[1], s_ref.at[2]
    adjs = (a0, a1, a2)
    for f in range(fields):
        adjs[f][...] = jnp.zeros_like(a0)

    count = cell.shape[0]

    def pick(i, carry):
        for j in range(8):
            r = i * 8 + j
            at = cell[r]
            m0[pl.ds(r, 1), :] = cosine[r] * s0[pl.ds(at, 1), :] + sine[r] * s1[pl.ds(at, 1), :]
            m1[pl.ds(r, 1), :] = s2[pl.ds(at, 1), :]
        return carry

    lax.fori_loop(0, count // 8, pick, 0)

    def weigh(i, total):
        at = pl.ds(pl.multiple_of(i * 8, 8), 8)
        first = (i * 8 // most) * (most + 1) + (i * 8) % most
        slot = pl.ds(first, 8)
        d0 = m0[at, :] - rows_ref[slot, 0, :]
        d1 = m1[at, :] - rows_ref[slot, 1, :]
        w0 = rows_ref[slot, 2, :] * d0
        w1 = rows_ref[slot, 3, :] * d1
        m0[at, :] = w0
        m1[at, :] = w1
        return total + (w0 * d0 + w1 * d1)

    obs[...] = lax.fori_loop(0, count // 8, weigh, jnp.zeros((8, w), F32))

    def push(i, carry):
        for j in range(8):
            r = i * 8 + j
            at = pl.ds(cell[r], 1)
            w0 = m0[pl.ds(r, 1), :]
            a0[at, :] = a0[at, :] + cosine[r] * w0
            a1[at, :] = a1[at, :] + sine[r] * w0
            a2[at, :] = a2[at, :] + m1[pl.ds(r, 1), :]
        return carry

    lax.fori_loop(0, count // 8, push, 0)
    for f in range(fields):
        grown = adjs[f]

        def scale_rows(y, carry):
            at = pl.ds(pl.multiple_of(y * a, a), a)
            adj[f, y] = grown[at, :] * spread[f, pl.ds(y, 1), :]
            return carry

        lax.fori_loop(0, b, scale_rows, 0)


def observe(cell, cosine, sine, state, spread, rows, most):
    f, b, w = spread.shape
    cells = state.shape[1]
    smem = pl.BlockSpec(memory_space=pltpu.SMEM)
    vmem = pl.BlockSpec(memory_space=pltpu.VMEM)
    return pl.pallas_call(
        functools.partial(observe_kernel, most),
        in_specs=[smem] * 3 + [vmem] * 3,
        out_specs=(vmem, vmem),
        out_shape=(
            jax.ShapeDtypeStruct((f, b, cells // b, w), F32),
            jax.ShapeDtypeStruct((8, w), F32),
        ),
        scratch_shapes=[pltpu.VMEM((cells, w), F32)] * 3
        + [pltpu.VMEM((cell.shape[0], w), F32)] * 2,
        compiler_params=params(),
        name="observe",
    )(cell, cosine, sine, state, spread, rows)


def gradient_kernel(x_ref, vert, c_ref, out, flat):
    b, a, w = x_ref.shape[1:]
    pitch = b + 8
    v = vert[0]
    for j in range(b // 2):
        x = jnp.concatenate([x_ref[0, 2 * j], x_ref[0, 2 * j + 1]], axis=1)
        r = mix_levels(v, x)
        flat[pl.ds(2 * j, a, stride=pitch), :] = r[:, :w]
        flat[pl.ds(2 * j + 1, a, stride=pitch), :] = r[:, w:]
    for s in range(a):
        out[0, s] = c_ref[0, s] + flat[s * pitch : s * pitch + b, :]


def gradient_of(x, vert, control):
    f, b, a, w = x.shape
    rows = 16
    tall = pl.BlockSpec((1, a, rows, w), lambda i, j: (i, 0, j, 0))
    return pl.pallas_call(
        gradient_kernel,
        grid=(f, b // rows),
        in_specs=[
            pl.BlockSpec((1, rows, a, w), lambda i, j: (i, j, 0, 0)),
            pl.BlockSpec((1, 2 * a, 2 * a), lambda i, j: (i, 0, 0)),
            tall,
        ],
        out_specs=tall,
        out_shape=jax.ShapeDtypeStruct(control.shape, F32),
        scratch_shapes=[pltpu.VMEM((a * (rows + 8), w), F32)],
        compiler_params=params(),
        name="gradient",
    )(x, vert, control)


def vertical_parts(v):
    high = lax.reduce_precision(v, 8, 7)
    low = lax.reduce_precision(v - high, 8, 7)
    both = jnp.concatenate([high, low], axis=1)
    return jnp.concatenate([both, both], axis=2).astype(BF16)


def body(
    control, spread, kernel_east, kernel_north, vertical,
    tile_owner, gate_level, tile_row, beam_azimuth, innovation, obs_weight,
):
    tiles = lax.axis_size("gx") * lax.axis_size("gy")
    most = 2 * tile_owner.shape[0] // tiles
    levels = control.shape[1]
    axes = ("gx", "gy")

    rows = pack_rows(
        tile_owner, gate_level, tile_row, beam_azimuth, innovation, obs_weight, tiles, most
    )
    rows = lax.all_to_all(rows, axes, split_axis=0, concat_axis=0, tiled=True)
    labels = rows.reshape(tiles, most + 1, 4, -1)[:, most, :3, :most]
    vert = vertical_parts(vertical)
    vert_back = vertical_parts(jnp.swapaxes(vertical, 1, 2))
    state, square = sweep(True, control, kernel_east, kernel_north, vert, spread)
    cell = (labels[:, 1] * levels + labels[:, 0]).astype(jnp.int32).reshape(-1)
    angle = labels[:, 2].reshape(-1) * (2.0 * math.pi / 360.0)
    adj, obs = observe(
        cell,
        jnp.cos(angle),
        jnp.sin(angle),
        state.reshape(state.shape[0], -1, state.shape[3]),
        spread,
        rows,
        most,
    )
    parts = jnp.stack([square, obs])
    smooth, totals = sweep(False, adj, kernel_east, kernel_north, parts, spread)
    counts = jnp.array([control.size * tiles, innovation.size * tiles], F32)
    cost = 0.5 * jnp.sum(totals, axis=(1, 2)) / counts
    return gradient_of(smooth, vert_back, control), cost


def solution(mesh):
    both = ("gx", "gy")
    placed = (
        P(None, None, "gy", "gx"),
        P(None, "gy", "gx"),
        P(),
        P(),
        P(),
        P(both),
        P(both),
        P(both),
        P(both),
        P(both, None, None),
        P(both, None, None),
    )
    return jax.shard_map(
        body,
        mesh=mesh,
        in_specs=placed,
        out_specs=(P(None, None, "gy", "gx"), P()),
        check_vma=False,
    )
```
